32 devices in a mesh: cfg: 2 (over core), seq: 8 (over z, x), wt: 2 (over y).
Axes of the slice: x: 2, y: 2, z: 4, core: 2. Of those that a mesh axis runs over, the one named last changes fastest.
Arguments:
- hidden: bfloat16 [2, 1280, 5120], P('cfg', 'seq'), may hold values from -1.5 to 1.5
- latent: float32 [1280, 64], P('seq', 'cfg'), may hold values from -6 to 6
- tenant_lengths: int32 [4], replicated, may hold values from 1 to 960, 1280 in all
- grid_positions: int32 [1280, 3], P('seq'), may hold values from 0 to 47
- text_kv: bfloat16 [2, 2, 2048, 3072], P(None, 'cfg', None, 'wt'), may hold values from -6 to 6
- text_lengths: int32 [2, 4], P('cfg'), may hold values from 1 to 512
- w_query: bfloat16 [5120, 3072], P(('cfg', 'seq'), 'wt'), may hold values from -0.078125 to 0.078125
- w_key: bfloat16 [5120, 3072], P(('cfg', 'seq'), 'wt'), may hold values from -0.078125 to 0.078125
- w_value: bfloat16 [5120, 3072], P(('cfg', 'seq'), 'wt'), may hold values from -0.078125 to 0.078125
- w_out: bfloat16 [5120, 3072], P(('cfg', 'seq'), 'wt'), may hold values from -0.109375 to 0.109375
- w_cross_query: bfloat16 [5120, 3072], P(('cfg', 'seq'), 'wt'), may hold values from -0.078125 to 0.078125
- w_cross_out: bfloat16 [5120, 3072], P(('cfg', 'seq'), 'wt'), may hold values from -0.109375 to 0.109375
- w_head: bfloat16 [5120, 64], replicated, may hold values from -0.078125 to 0.078125
- guidance: float32 [1], replicated, may hold values from 3 to 7
- step_size: float32 [1], replicated, may hold values from -0.3 to -0.05
Outputs:
- hidden_out: bfloat16 [2, 1280, 5120], P('cfg', 'seq', 'wt')
- latent_next: float32 [1280, 64], P('seq', 'cfg')
The draws below stay inside these ranges and needn't reach their ends.
Inputs may be any that keep to these rules, and one draw needn't show every extreme that they name: `tenant_lengths`: the lengths sum to 1280; the largest is exactly 960.
All inputs are finite; a program needn't handle non-finite values.
Results may differ from the reference program's by a relative error of at most 0.013.
Values may be sent and summed in bfloat16 or wider, within the bound.
A program may use at most 192 MiB of HBM per device.

```python
import math
import jax
import jax.numpy as jnp
import numpy as np
from jax import lax

D = 5120
HEADS = 24
HD = 128
TEXT = 512
TENANTS = 4
OUTC = 64
C = 3072
TOKENS = 1280
N_WT = 2


def set_ends(result, own_key, least, high):
    longest = result.shape.index(max(result.shape))
    spots = []
    for shift in (0, 1):
        where = [jax.random.randint(jax.random.fold_in(own_key, axis), (), 0, length) for axis, length in enumerate(result.shape)]
        where[longest] = (where[longest] + shift) % result.shape[longest]
        spots.append(tuple(where))
    return result.at[spots[0]].set(least).at[spots[1]].set(high)


def block_levels(key, extent, split, smallest, top_value):
    loudness, own = 1.0, jax.random.fold_in(key, 6)
    for dim, blocks in split:
        heights = jnp.exp(jax.random.uniform(jax.random.fold_in(own, dim), (blocks,), jnp.float32, smallest / len(split), top_value / len(split)))
        loudness = loudness * jnp.repeat(heights, extent[dim] // blocks).reshape([-1 if axis == dim else 1 for axis in range(len(extent))])
    return loudness


def length_profile(amount, total, limit, slope):
    weights = [(1 << 20) // math.isqrt(grade ** slope) + 1 for grade in range(2, amount + 1)]
    rest, given = total - limit - (amount - 1), [1] * (amount - 1)
    while rest > 0:
        free = [i for i in range(amount - 1) if given[i] < limit]
        whole, remaining = sum([weights[i] for i in free]), rest
        for i in free:
            addition = min(limit - given[i], max(1, remaining * weights[i] // whole), rest)
            given[i] = given[i] + addition
            rest = rest - addition
    return np.array([limit] + given)


def uneven(rng, count, total, bound, lean):
    if count == 2:
        one = jax.random.randint(rng, (), max(1, total - bound), min(bound, total - 1) + 1)
        return jnp.stack([one, total - one])
    lengths = jnp.asarray(length_profile(count, total, bound, lean), jnp.int32)
    twos = (count - 1) // 2
    giver, receiver = lengths[1:1 + 2 * twos:2], lengths[2:2 + 2 * twos:2]
    margin = jnp.minimum(giver - 1, bound - receiver)
    moved = jax.random.randint(jax.random.fold_in(rng, 1), (twos,), 0, 1 << 20) % (margin + 1)
    lengths = lengths.at[1:1 + 2 * twos:2].set(giver - moved).at[2:2 + 2 * twos:2].set(receiver + moved)
    return lengths[jax.random.permutation(jax.random.fold_in(rng, 2), count)]


def normal_values(stream_key, shape, deviation, bound, shards=(), kind=jnp.bfloat16):
    level = block_levels(stream_key, shape, shards, -0.22, 0.18) if shards else 1.0
    values = jax.random.normal(stream_key, shape, jnp.float32) * deviation * level
    return jnp.minimum(jnp.maximum(values, -bound), bound).astype(kind)


def setup_inputs(seed: int = 0) -> dict:
    splits = jax.random.split(jax.random.key(seed), 16)
    return {
        "hidden": normal_values(splits[0], (2, TOKENS, D), 0.25, 1.5, ((0, 2), (1, 8))),
        "latent": normal_values(splits[1], (TOKENS, OUTC), 1.0, 6.0, ((0, 8), (1, 2)), jnp.float32),
        "tenant_lengths": uneven(splits[2], TENANTS, TOKENS, 3 * TOKENS // 4, 2).astype(jnp.int32),
        "grid_positions": set_ends(jax.random.randint(splits[3], (TOKENS, 3), 0, 48), jax.random.fold_in(splits[3], 1), 0, 47).astype(jnp.int32),
        "text_kv": normal_values(splits[4], (2, 2, TENANTS * TEXT, C), 1.0, 6.0, ((1, 2), (3, 2))),
        "text_lengths": set_ends(jax.random.randint(splits[5], (2, TENANTS), 1, TEXT + 1), jax.random.fold_in(splits[5], 1), 1, TEXT).astype(jnp.int32),
        "w_query": normal_values(splits[6], (D, C), D ** -0.5, 0.078125, ((0, 16), (1, 2))),
        "w_key": normal_values(splits[7], (D, C), D ** -0.5, 0.078125, ((0, 16), (1, 2))),
        "w_value": normal_values(splits[8], (D, C), D ** -0.5, 0.078125, ((0, 16), (1, 2))),
        "w_out": normal_values(splits[9], (D, C), C ** -0.5, 0.109375, ((0, 16), (1, 2))),
        "w_cross_query": normal_values(splits[10], (D, C), D ** -0.5, 0.078125, ((0, 16), (1, 2))),
        "w_cross_out": normal_values(splits[11], (D, C), C ** -0.5, 0.109375, ((0, 16), (1, 2))),
        "w_head": normal_values(splits[12], (D, OUTC), D ** -0.5, 0.078125),
        "guidance": jnp.clip(jax.random.uniform(splits[13], (1,), jnp.float32, 3.0, 7.0), 3.0, 7.0),
        "step_size": jnp.clip(jax.random.uniform(splits[14], (1,), jnp.float32, -0.3, -0.05), -0.3, -0.05),
    }


epsilon = 1e-06

def layer_norm(inputs):
    average = lax.optimization_barrier(jnp.mean(inputs, axis=-1, keepdims=True))
    centred = inputs - average
    variance = lax.optimization_barrier(jnp.mean(centred * centred, axis=-1, keepdims=True))
    return centred * lax.rsqrt(variance + epsilon)

def head_norm(inputs, head_dim):
    shaped = inputs.reshape(inputs.shape[:-1] + (inputs.shape[-1] // head_dim, head_dim))
    return shaped * lax.rsqrt(lax.optimization_barrier(jnp.mean(shaped * shaped, axis=-1, keepdims=True)) + epsilon)

def rotary(inputs, grid):
    head_dim = inputs.shape[-1]
    sixth_part = head_dim // 6
    angle_parts = []
    for dim_index, span_width in enumerate((head_dim - 4 * sixth_part, 2 * sixth_part, 2 * sixth_part)):
        exponent = jnp.arange(0, span_width, 2).astype(jnp.float32) / span_width
        frequency = 1.0 / 10000.0 ** exponent
        angle_parts.append(grid[:, dim_index:dim_index + 1].astype(jnp.float32) * frequency[None, :])
    angles = jnp.concatenate(angle_parts, axis=1)[:, None, :]
    paired = inputs.reshape(inputs.shape[:-1] + (head_dim // 2, 2))
    even_part = paired[..., 0]
    odd_part = paired[..., 1]
    cosine = jnp.cos(angles)
    sinus = jnp.sin(angles)
    rotated = jnp.stack([even_part * cosine - odd_part * sinus, even_part * sinus + odd_part * cosine], axis=-1)
    return rotated.reshape(inputs.shape)

def attention(queries, keys, values, allowed):
    score_scale = 1.0 / math.sqrt(queries.shape[-1])

    def one_head(operands):
        query_head, key_head, value_head = operands
        scores = jnp.dot(query_head, key_head.T, preferred_element_type=jnp.float32) * score_scale
        weights = jnp.where(allowed, jnp.exp(scores), 0.0).astype(jnp.bfloat16)
        running_sum = lax.optimization_barrier(jnp.sum(weights.astype(jnp.float32), axis=1))
        summed = jnp.dot(weights, value_head, preferred_element_type=jnp.float32)
        return (summed / running_sum[:, None]).astype(jnp.bfloat16)
    outputs = lax.map(one_head, (jnp.swapaxes(queries, 0, 1), jnp.swapaxes(keys, 0, 1), jnp.swapaxes(values, 0, 1)))
    return jnp.swapaxes(outputs, 0, 1).reshape(queries.shape[0], -1)

def grouped_project(mixed, weight):
    group_cols = weight.shape[1] // N_WT
    running_sum = jnp.zeros((mixed.shape[0], weight.shape[0]), jnp.float32)
    for number in range(N_WT):
        lower = number * group_cols
        partial_value = jnp.dot(mixed[:, lower:lower + group_cols], weight[:, lower:lower + group_cols].T, preferred_element_type=jnp.float32)
        rounded = lax.optimization_barrier(partial_value.astype(jnp.bfloat16))
        running_sum = running_sum + rounded.astype(jnp.float32)
    return running_sum

def reference(hidden, latent, tenant_lengths, grid_positions, text_kv, text_lengths, w_query, w_key, w_value, w_out, w_cross_query, w_cross_out, w_head, guidance, step_size):
    ends = jnp.cumsum(tenant_lengths)
    positions = jnp.arange(TOKENS, dtype=jnp.int32)
    tenant = lax.optimization_barrier(jnp.sum((positions[:, None] >= ends[None, :]).astype(jnp.int32), axis=1))
    same_tenant = tenant[:, None] == tenant[None, :]
    text_index = jnp.arange(TENANTS * TEXT, dtype=jnp.int32)
    text_tenant = text_index // TEXT
    text_slot = text_index % TEXT
    tenant_table = text_tenant[:, None] == jnp.arange(TENANTS, dtype=jnp.int32)[None, :]
    outputs = []
    velocities = []
    for half in range(2):
        state = hidden[half].astype(jnp.float32)
        normed = layer_norm(state).astype(jnp.bfloat16)
        queries = rotary(head_norm(jnp.dot(normed, w_query, preferred_element_type=jnp.float32), HD), grid_positions).astype(jnp.bfloat16)
        keys = rotary(head_norm(jnp.dot(normed, w_key, preferred_element_type=jnp.float32), HD), grid_positions).astype(jnp.bfloat16)
        values = jnp.dot(normed, w_value, preferred_element_type=jnp.float32).astype(jnp.bfloat16)
        values = values.reshape(TOKENS, HEADS, HD)
        mixed = attention(queries, keys, values, same_tenant)
        state = state + grouped_project(mixed, w_out)
        normed = layer_norm(state).astype(jnp.bfloat16)
        cross_queries = head_norm(jnp.dot(normed, w_cross_query, preferred_element_type=jnp.float32), HD).astype(jnp.bfloat16)
        text_keys = head_norm(text_kv[0, half].astype(jnp.float32), HD).astype(jnp.bfloat16)
        text_values = text_kv[1, half].reshape(TENANTS * TEXT, HEADS, HD)
        live_length = lax.optimization_barrier(jnp.sum(jnp.where(tenant_table, text_lengths[half][None, :], 0), axis=1))
        live = text_slot < live_length
        allowed = (tenant[:, None] == text_tenant[None, :]) & live[None, :]
        mixed = attention(cross_queries, text_keys, text_values, allowed)
        state = state + grouped_project(mixed, w_cross_out)
        outputs.append(state.astype(jnp.bfloat16))
        velocities.append(jnp.dot(layer_norm(state).astype(jnp.bfloat16), w_head, preferred_element_type=jnp.float32))
    guided = velocities[1] + guidance[0] * (velocities[0] - velocities[1])
    return (jnp.stack(outputs), latent + step_size[0] * guided)
```

```python
import math

import jax
import jax.numpy as jnp
import numpy as np
from jax import lax
from jax.sharding import Mesh
from jax.sharding import PartitionSpec as P

HD = 128
TEXT = 512
TENANTS = 4
EPS = 1e-06
BF = jnp.bfloat16
F32 = jnp.float32


def flip(block, axis):
    return lax.ppermute(block, axis, [(0, 1), (1, 0)])


def rotary_tables():
    sixth = HD // 6
    table = np.zeros((3, HD), np.float32)
    lane = 0
    for column, span in enumerate((HD - 4 * sixth, 2 * sixth, 2 * sixth)):
        exponent = np.arange(0, span, 2).astype(np.float32) / np.float32(span)
        frequency = (1.0 / 10000.0**exponent).astype(np.float32)
        table[column, lane : lane + span] = np.repeat(frequency, 2)
        lane += span
    swap = np.zeros((HD, HD), np.float32)
    for pair in range(0, HD, 2):
        swap[pair + 1, pair] = -1.0
        swap[pair, pair + 1] = 1.0
    return table, swap


def head_scale(shaped):
    return lax.rsqrt(jnp.mean(shaped * shaped, axis=-1, keepdims=True) + EPS)


def attend(queries, keys, values, allowed):
    scores = jnp.einsum("qhd,khd->hqk", queries, keys, preferred_element_type=F32)
    scores = scores * (1.0 / math.sqrt(queries.shape[-1]))
    weights = jnp.where(allowed[None], jnp.exp(scores), 0.0).astype(BF)
    summed = jnp.einsum("hqk,khd->qhd", weights, values, preferred_element_type=F32)
    totals = jnp.sum(weights.astype(F32), axis=2).T
    return (summed / totals[..., None]).astype(BF).reshape(queries.shape[0], -1)


def on_device(
    hidden,
    latent,
    tenant_lengths,
    grid_positions,
    text_kv,
    text_lengths,
    w_query,
    w_key,
    w_value,
    w_out,
    w_cross_query,
    w_cross_out,
    w_head,
    guidance,
    step_size,
):
    halves, groups, parts, columns = (lax.axis_size(a) for a in ("cfg", "z", "t", "wt"))
    half_index, z_index, t_index, wt_index = (
        lax.axis_index(a) for a in ("cfg", "z", "t", "wt")
    )
    tok, width = hidden.shape[1:]
    rows = groups * tok
    local_cols = w_query.shape[1]
    my_cols = local_cols // groups
    heads = my_cols // HD
    paired = halves == 2 and parts == 2
    block = w_query.shape[0]
    ends = jnp.cumsum(tenant_lengths)

    def tenant_of(indices):
        return jnp.sum((indices[:, None] >= ends[None, :]).astype(jnp.int32), axis=1)

    def wide(w):
        if not paired:
            return lax.all_gather(w, ("cfg", "t"), axis=0, tiled=True)
        two = jnp.concatenate([w, flip(w, "t")], axis=0)
        return jnp.concatenate([two, flip(two, "cfg")], axis=0)

    def local_order(x):
        if not paired:
            return x
        x = jnp.where(t_index == 1, x[..., ::-1, :], x)
        return jnp.where(half_index == 1, x[..., ::-1, :, :], x)

    def over_groups(x):
        return x if groups == 1 else lax.all_to_all(x, "z", 0, 0, tiled=True)

    def join_groups(x):
        if groups == 1:
            return x
        x = lax.all_gather(x, "z", axis=0)
        return jnp.swapaxes(x, 0, 1).reshape(rows, local_cols)

    def sum_groups(x):
        if groups == 1:
            return x
        return lax.psum_scatter(x, "z", scatter_dimension=0, tiled=True)

    def to_groups(x, n):
        return jnp.swapaxes(x.reshape(x.shape[0], groups, n), 0, 1)

    def both_columns(terms):
        terms = terms.astype(BF)
        if columns == 1:
            return terms.astype(F32)
        if columns == 2:
            return terms.astype(F32) + flip(terms, "wt").astype(F32)
        return lax.psum(terms, "wt").astype(F32)

    wide_query, wide_key, wide_value = wide(w_query), wide(w_key), wide(w_value)
    wide_out, wide_cross, wide_cross_out = wide(w_out), wide(w_cross_query), wide(w_cross_out)

    own = hidden[0]
    sliced = local_order(
        jnp.transpose(own.reshape(tok, halves, groups, parts, block), (2, 0, 1, 3, 4))
    ).reshape(rows, width // groups)
    sliced = over_groups(sliced).astype(F32)
    own = own.astype(F32)
    mean = jnp.mean(own, axis=-1, keepdims=True)
    centred = own - mean
    scale = lax.rsqrt(jnp.mean(centred * centred, axis=-1, keepdims=True) + EPS)
    facts = jnp.concatenate([mean, scale, grid_positions.astype(F32)], axis=1)
    if groups > 1:
        facts = lax.all_gather(facts, "z", axis=0, tiled=True)
    normed = ((sliced - facts[:, 0:1]) * facts[:, 1:2]).astype(BF)

    projected = jnp.concatenate(
        [
            to_groups(jnp.dot(normed, w, preferred_element_type=F32).astype(BF), my_cols)
            for w in (wide_query, wide_key, wide_value)
        ],
        axis=2,
    )
    projected = sum_groups(projected.reshape(groups * rows, 3 * my_cols))

    table, swap = rotary_tables()
    angles = (
        facts[:, 2:3] * table[0][None] + facts[:, 3:4] * table[1][None] + facts[:, 4:5] * table[2][None]
    )
    cosine, sinus = jnp.cos(angles)[:, None, :], jnp.sin(angles)[:, None, :]

    def rotated(x):
        shaped = x.reshape(rows, heads, HD)
        swapped = jnp.einsum("thd,de->the", shaped, jnp.asarray(swap, BF), preferred_element_type=F32)
        shaped = shaped.astype(F32)
        return ((shaped * cosine + swapped * sinus) * head_scale(shaped)).astype(BF)

    queries = rotated(projected[:, :my_cols])
    keys = rotated(projected[:, my_cols : 2 * my_cols]).reshape(rows, my_cols)
    key_value = jnp.concatenate([keys, projected[:, 2 * my_cols :]], axis=1)

    base = (jnp.arange(groups, dtype=jnp.int32) * parts * tok)[:, None] + jnp.arange(
        tok, dtype=jnp.int32
    )[None]
    base = base.reshape(-1)
    my_tenant = tenant_of(base + t_index * tok)
    if parts == 2:
        key_value = jnp.concatenate([key_value, flip(key_value, "t")], axis=0)
        key_tenant = jnp.concatenate([my_tenant, tenant_of(base + (1 - t_index) * tok)])
    else:
        key_value = lax.all_gather(key_value, "t", axis=0, tiled=True)
        key_tenant = tenant_of(
            (jnp.arange(parts, dtype=jnp.int32)[:, None] * tok + base[None]).reshape(-1)
        )
    mixed = attend(
        queries,
        key_value[:, :my_cols].reshape(-1, heads, HD),
        key_value[:, my_cols:].reshape(-1, heads, HD),
        my_tenant[:, None] == key_tenant[None, :],
    )

    def project_out(mixed, weight):
        return lax.dot_general(
            join_groups(mixed), weight, (((1,), (1,)), ((), ())), preferred_element_type=F32
        )

    state = sliced + both_columns(project_out(mixed, wide_out))

    shifted = state - facts[:, 0:1]
    sums = jnp.concatenate(
        [jnp.sum(shifted, axis=1, keepdims=True), jnp.sum(shifted * shifted, axis=1, keepdims=True)],
        axis=1,
    )
    if groups > 1:
        sums = lax.psum(sums, "z")
    sums = sums / width
    scale = lax.rsqrt(jnp.maximum(sums[:, 1:2] - sums[:, 0:1] ** 2, 0.0) + EPS)
    normed = ((shifted - sums[:, 0:1]) * scale).astype(BF)
    crossed = jnp.dot(normed, wide_cross, preferred_element_type=F32).astype(BF)
    crossed = to_groups(crossed, my_cols).reshape(groups, rows, my_cols)
    crossed = jnp.sum(
        over_groups(crossed.reshape(groups * rows, my_cols))
        .reshape(groups, rows, my_cols)
        .astype(F32),
        axis=0,
    )
    shaped = crossed.reshape(rows, heads, HD)
    cross_queries = (shaped * head_scale(shaped)).astype(BF)
    text = lax.dynamic_slice_in_dim(text_kv[:, 0], z_index * my_cols, my_cols, 2)
    text_keys = text[0].reshape(-1, heads, HD).astype(F32)
    text_keys = (text_keys * head_scale(text_keys)).astype(BF)
    text_values = text[1].reshape(-1, heads, HD)
    text_index = jnp.arange(text_kv.shape[2], dtype=jnp.int32)
    text_tenant = text_index // TEXT
    table = text_tenant[:, None] == jnp.arange(TENANTS, dtype=jnp.int32)[None, :]
    live_length = jnp.sum(jnp.where(table, text_lengths[0][None, :], 0), axis=1)
    allowed = (my_tenant[:, None] == text_tenant[None, :]) & (text_index % TEXT < live_length)[None]
    cross_mixed = attend(cross_queries, text_keys, text_values, allowed)
    terms = project_out(cross_mixed, wide_cross_out)

    head_rows = w_head.reshape(halves, groups, parts, block, -1)
    head_rows = lax.dynamic_index_in_dim(head_rows, z_index, 1, keepdims=False)
    if paired:
        head_rows = jnp.where(t_index == 1, head_rows[:, ::-1], head_rows)
        head_rows = jnp.where(half_index == 1, head_rows[::-1], head_rows)
    channels = head_rows.shape[-1]
    head_rows = head_rows.reshape(-1, channels)

    final = state + both_columns(terms)
    out_width = width // columns
    if groups == 1:
        hidden_out = lax.dynamic_slice_in_dim(final.astype(BF), wt_index * out_width, out_width, 1)
    else:
        leaving = final.astype(BF).reshape(groups, tok, halves, parts, block)
        if paired:
            leaving = jnp.where(t_index == 1, leaving[:, :, :, ::-1], leaving)
            leaving = jnp.where(half_index == 1, leaving[:, :, ::-1], leaving)
        if columns == halves:
            leaving = lax.dynamic_index_in_dim(leaving, wt_index, 2, keepdims=True)
        leaving = over_groups(leaving)
        hidden_out = jnp.transpose(leaving, (1, 2, 0, 3, 4)).reshape(tok, -1)
        if columns != halves:
            hidden_out = lax.dynamic_slice_in_dim(hidden_out, wt_index * out_width, out_width, 1)

    shifted = final - facts[:, 0:1]
    sums = jnp.concatenate(
        [
            jnp.dot(shifted.astype(BF), head_rows, preferred_element_type=F32),
            jnp.sum(shifted, axis=1, keepdims=True),
            jnp.sum(shifted * shifted, axis=1, keepdims=True),
        ],
        axis=1,
    )
    if groups > 1:
        sums = jnp.sum(over_groups(sums).reshape(groups, tok, -1), axis=0)
    mean = sums[:, channels : channels + 1] / width
    square = sums[:, channels + 1 :] / width
    scale = lax.rsqrt(jnp.maximum(square - mean * mean, 0.0) + EPS)
    totals = jnp.sum(w_head.astype(F32), axis=0)[None]
    velocity = (sums[:, :channels] - mean * totals) * scale

    channel_half = latent.shape[1]
    outgoing = lax.dynamic_slice_in_dim(velocity, (1 - half_index) * channel_half, channel_half, 1)
    partner = flip(outgoing, "cfg")
    own_part = lax.dynamic_slice_in_dim(velocity, half_index * channel_half, channel_half, 1)
    conditional = jnp.where(half_index == 0, own_part, partner)
    null_text = jnp.where(half_index == 0, partner, own_part)
    latent_next = latent + step_size[0] * (null_text + guidance[0] * (conditional - null_text))
    return (hidden_out[None], latent_next)


def solution(mesh):
    halves, seq, columns = (mesh.shape[a] for a in ("cfg", "seq", "wt"))

    def run(*args):
        heads_here = args[6].shape[1] // columns // HD
        groups = math.gcd(heads_here, seq)
        fine = Mesh(
            mesh.devices.reshape(halves, groups, seq // groups, columns), ("cfg", "z", "t", "wt")
        )
        seq_axes = ("z", "t")
        weight = P(("cfg", "z", "t"), "wt")
        return jax.shard_map(
            on_device,
            mesh=fine,
            in_specs=(
                P("cfg", seq_axes, None),
                P(seq_axes, "cfg"),
                P(),
                P(seq_axes, None),
                P(None, "cfg", None, "wt"),
                P("cfg", None),
                weight,
                weight,
                weight,
                weight,
                weight,
                weight,
                P(),
                P(),
                P(),
            ),
            out_specs=(P("cfg", seq_axes, "wt"), P(seq_axes, "cfg")),
            check_vma=False,
        )(*args)

    return run
```

```python
import math

import jax
import jax.numpy as jnp
import numpy as np
from jax import lax
from jax.sharding import Mesh
from jax.sharding import PartitionSpec as P

HD = 128
TEXT = 512
TENANTS = 4
EPS = 1e-06
CHUNKS = 2
BF = jnp.bfloat16
F32 = jnp.float32


def flip(block, axis):
    return lax.ppermute(block, axis, [(0, 1), (1, 0)])


def rotary_tables():
    sixth = HD // 6
    table = np.zeros((3, HD), np.float32)
    lane = 0
    for column, span in enumerate((HD - 4 * sixth, 2 * sixth, 2 * sixth)):
        exponent = np.arange(0, span, 2).astype(np.float32) / np.float32(span)
        frequency = (1.0 / 10000.0**exponent).astype(np.float32)
        table[column, lane : lane + span] = np.repeat(frequency, 2)
        lane += span
    swap = np.zeros((HD, HD), np.float32)
    for pair in range(0, HD, 2):
        swap[pair + 1, pair] = -1.0
        swap[pair, pair + 1] = 1.0
    return table, swap


def head_scale(shaped):
    return lax.rsqrt(jnp.mean(shaped * shaped, axis=-1, keepdims=True) + EPS)


def attend(queries, keys, values, allowed):
    scores = jnp.einsum("qhd,khd->hqk", queries, keys, preferred_element_type=F32)
    scores = scores * (1.0 / math.sqrt(queries.shape[-1]))
    weights = jnp.where(allowed[None], jnp.exp(scores), 0.0).astype(BF)
    summed = jnp.einsum("hqk,khd->qhd", weights, values, preferred_element_type=F32)
    totals = jnp.sum(weights.astype(F32), axis=2).T
    return (summed / totals[..., None]).astype(BF).reshape(queries.shape[0], -1)


def on_device(
    hidden,
    latent,
    tenant_lengths,
    grid_positions,
    text_kv,
    text_lengths,
    w_query,
    w_key,
    w_value,
    w_out,
    w_cross_query,
    w_cross_out,
    w_head,
    guidance,
    step_size,
):
    halves, groups, parts, columns = (lax.axis_size(a) for a in ("cfg", "z", "t", "wt"))
    half_index, z_index, t_index, wt_index = (
        lax.axis_index(a) for a in ("cfg", "z", "t", "wt")
    )
    tok, width = hidden.shape[1:]
    rows = groups * tok
    local_cols = w_query.shape[1]
    my_cols = local_cols // groups
    heads = my_cols // HD
    paired = halves == 2 and parts == 2
    block = w_query.shape[0]
    ends = jnp.cumsum(tenant_lengths)

    def tenant_of(indices):
        return jnp.sum((indices[:, None] >= ends[None, :]).astype(jnp.int32), axis=1)

    def ordered(mine, other, index):
        return jnp.where(
            index == 0, jnp.concatenate([mine, other]), jnp.concatenate([other, mine])
        )

    def wide(w):
        if not paired:
            return lax.all_gather(w, ("cfg", "t"), axis=0, tiled=True)
        two = ordered(w, flip(w, "t"), t_index)
        return ordered(two, flip(two, "cfg"), half_index)

    def over_groups(x):
        return x if groups == 1 else lax.all_to_all(x, "z", 0, 0, tiled=True)

    def join_groups(x):
        if groups == 1:
            return x
        x = lax.all_gather(x, "z", axis=0)
        return jnp.swapaxes(x, 0, 1).reshape(x.shape[1], local_cols)

    def sum_at_owner(x):
        if groups == 1:
            return x[0].astype(F32)
        return jnp.sum(lax.all_to_all(x, "z", 0, 0).astype(F32), axis=0)

    def sum_groups(x):
        if groups == 1:
            return x
        return lax.psum_scatter(x, "z", scatter_dimension=0, tiled=True)

    def to_groups(x, n):
        return jnp.swapaxes(x.reshape(x.shape[0], groups, n), 0, 1)

    def both_columns(terms):
        terms = terms.astype(BF)
        if columns == 1:
            return terms.astype(F32)
        if columns == 2:
            return terms.astype(F32) + flip(terms, "wt").astype(F32)
        return lax.psum(terms, "wt").astype(F32)

    wide_query, wide_key, wide_value = wide(w_query), wide(w_key), wide(w_value)
    wide_out, wide_cross, wide_cross_out = wide(w_out), wide(w_cross_query), wide(w_cross_out)

    chunks = CHUNKS if groups > 1 and tok % (CHUNKS * 16) == 0 else 1
    part = tok // chunks
    chunk_rows = rows // chunks

    def by_chunk(x):
        shape = (groups, chunks, part) + x.shape[2:]
        return jnp.swapaxes(x.reshape(shape), 0, 1).reshape((rows,) + x.shape[2:])

    own = hidden[0].astype(F32)
    mean = jnp.mean(own, axis=-1, keepdims=True)
    centred = own - mean
    scale = lax.rsqrt(jnp.mean(centred * centred, axis=-1, keepdims=True) + EPS)
    facts = jnp.concatenate([mean, scale, grid_positions.astype(F32)], axis=1)
    slice_width = width // groups
    if groups == 1:
        sliced = own
    else:
        high = lax.reduce_precision(facts, 8, 7)
        middle = lax.reduce_precision(facts - high, 8, 7)
        low = facts - high - middle
        extra = jnp.concatenate([high, middle, low], axis=1).astype(BF)
        extra = jnp.pad(extra, ((0, 0), (0, 128 - extra.shape[1])))
        features = hidden[0].reshape(tok, halves, groups, slice_width // halves)
        features = jnp.concatenate(
            [features[:, half] for half in range(halves)]
            + [jnp.broadcast_to(extra[:, None], (tok, groups, 128))],
            axis=2,
        )
        arrived = lax.all_to_all(jnp.swapaxes(features, 0, 1), "z", 0, 0)
        arrived = by_chunk(arrived).astype(F32)
        sliced = arrived[:, :slice_width]
        extra = arrived[:, slice_width : slice_width + 15]
        facts = extra[:, 0:5] + extra[:, 5:10] + extra[:, 10:15]
    normed = ((sliced - facts[:, 0:1]) * facts[:, 1:2]).astype(BF)

    def project(w):
        return to_groups(jnp.dot(normed, w, preferred_element_type=F32).astype(BF), my_cols)

    projected_keys = sum_at_owner(project(wide_key)).astype(BF)
    projected = jnp.concatenate([project(wide_query), project(wide_value)], axis=2)
    projected = sum_groups(projected.reshape(groups * rows, 2 * my_cols))

    table, swap = rotary_tables()
    angles = (
        facts[:, 2:3] * table[0][None] + facts[:, 3:4] * table[1][None] + facts[:, 4:5] * table[2][None]
    )
    cosine, sinus = jnp.cos(angles)[:, None, :], jnp.sin(angles)[:, None, :]

    def rotated(x):
        shaped = x.reshape(rows, heads, HD)
        swapped = jnp.einsum("thd,de->the", shaped, jnp.asarray(swap, BF), preferred_element_type=F32)
        shaped = shaped.astype(F32)
        return ((shaped * cosine + swapped * sinus) * head_scale(shaped)).astype(BF)

    keys = rotated(projected_keys).reshape(rows, my_cols)
    queries = rotated(projected[:, :my_cols])
    values = projected[:, my_cols:]

    base = jnp.arange(groups, dtype=jnp.int32)[:, None] * (parts * tok)
    base = by_chunk(base + jnp.arange(tok, dtype=jnp.int32)[None])
    my_tenant = tenant_of(base + t_index * tok)
    if parts == 2:
        keys = jnp.concatenate([keys, flip(keys, "t")], axis=0)
        values = jnp.concatenate([values, flip(values, "t")], axis=0)
        key_tenant = jnp.concatenate([my_tenant, tenant_of(base + (1 - t_index) * tok)])
    else:
        keys = lax.all_gather(keys, "t", axis=0, tiled=True)
        values = lax.all_gather(values, "t", axis=0, tiled=True)
        key_tenant = tenant_of(
            (jnp.arange(parts, dtype=jnp.int32)[:, None] * tok + base[None]).reshape(-1)
        )
    keys = keys.reshape(-1, heads, HD)
    values = values.reshape(-1, heads, HD)

    spans = [slice(i * chunk_rows, (i + 1) * chunk_rows) for i in range(chunks)]
    mixed = [
        attend(queries[i], keys, values, my_tenant[i][:, None] == key_tenant[None, :])
        for i in spans
    ]

    def project_out(mixed, weight):
        return lax.dot_general(
            join_groups(mixed), weight, (((1,), (1,)), ((), ())), preferred_element_type=F32
        )

    column_sums = jnp.dot(jnp.ones((8, slice_width), BF), wide_cross, preferred_element_type=F32)
    column_sums = sum_at_owner(column_sums[0].reshape(groups, 1, my_cols))

    text = lax.dynamic_slice_in_dim(text_kv[:, 0], z_index * my_cols, my_cols, 2)
    text_keys = text[0].reshape(-1, heads, HD).astype(F32)
    text_keys = (text_keys * head_scale(text_keys)).astype(BF)
    text_values = text[1].reshape(-1, heads, HD)
    text_index = jnp.arange(text_kv.shape[2], dtype=jnp.int32)
    text_tenant = text_index // TEXT
    slots = text_tenant[:, None] == jnp.arange(TENANTS, dtype=jnp.int32)[None, :]
    live_length = jnp.sum(jnp.where(slots, text_lengths[0][None, :], 0), axis=1)
    live = text_index % TEXT < live_length

    states, cross_mixed = [], []
    for i, block_mixed in zip(spans, mixed):
        shifted = (sliced[i] - facts[i, 0:1]) + both_columns(project_out(block_mixed, wide_out))
        states.append(shifted)
        sums = jnp.stack([jnp.sum(shifted, axis=1), jnp.sum(shifted * shifted, axis=1)])
        sums = sum_at_owner(jnp.broadcast_to(sums[None], (groups,) + sums.shape)) / width
        crossed = jnp.dot(shifted.astype(BF), wide_cross, preferred_element_type=F32).astype(BF)
        crossed = sum_at_owner(to_groups(crossed, my_cols))
        variance = jnp.maximum(sums[1] - sums[0] * sums[0], 0.0)[:, None, None]
        shaped = (crossed - sums[0][:, None] * column_sums).reshape(chunk_rows, heads, HD)
        square = jnp.mean(shaped * shaped, axis=-1, keepdims=True)
        cross_queries = (shaped * lax.rsqrt(square + EPS * (variance + EPS))).astype(BF)
        allowed = (my_tenant[i][:, None] == text_tenant[None, :]) & live[None]
        cross_mixed.append(attend(cross_queries, text_keys, text_values, allowed))

    channels = w_head.shape[1]
    head_rows = lax.dynamic_index_in_dim(
        w_head.reshape(halves, groups, parts * block, channels), z_index, 1, keepdims=False
    ).reshape(-1, channels)
    totals = jnp.sum(w_head.astype(F32), axis=0)[None]
    out_width = width // columns

    leaving, velocity = [], []
    for i, shifted, block_mixed in zip(spans, states, cross_mixed):
        shifted = shifted + both_columns(project_out(block_mixed, wide_cross_out))
        final = (shifted + facts[i, 0:1]).astype(BF)
        if groups == 1:
            leaving.append(lax.dynamic_slice_in_dim(final, wt_index * out_width, out_width, 1))
        else:
            final = final.reshape(groups, part, slice_width)
            if columns == halves:
                span = slice_width // halves
                final = lax.dynamic_slice_in_dim(final, wt_index * span, span, 2)
            final = jnp.swapaxes(lax.all_to_all(final, "z", 0, 0), 0, 1)
            if columns == halves:
                leaving.append(final.reshape(part, out_width))
            else:
                final = final.reshape(part, groups, halves, -1)
                final = jnp.swapaxes(final, 1, 2).reshape(part, width)
                leaving.append(
                    lax.dynamic_slice_in_dim(final, wt_index * out_width, out_width, 1)
                )
        sums = jnp.concatenate(
            [
                jnp.dot(shifted.astype(BF), head_rows, preferred_element_type=F32),
                jnp.sum(shifted, axis=1, keepdims=True),
                jnp.sum(shifted * shifted, axis=1, keepdims=True),
            ],
            axis=1,
        )
        sums = sum_at_owner(sums.reshape(groups, part, channels + 2))
        mean = sums[:, channels : channels + 1] / width
        variance = jnp.maximum(sums[:, channels + 1 :] / width - mean * mean, 0.0)
        velocity.append((sums[:, :channels] - mean * totals) * lax.rsqrt(variance + EPS))
    hidden_out = jnp.concatenate(leaving)
    velocity = jnp.concatenate(velocity)

    channel_half = latent.shape[1]
    outgoing = lax.dynamic_slice_in_dim(velocity, (1 - half_index) * channel_half, channel_half, 1)
    partner = flip(outgoing, "cfg")
    own_part = lax.dynamic_slice_in_dim(velocity, half_index * channel_half, channel_half, 1)
    conditional = jnp.where(half_index == 0, own_part, partner)
    null_text = jnp.where(half_index == 0, partner, own_part)
    latent_next = latent + step_size[0] * (null_text + guidance[0] * (conditional - null_text))
    return (hidden_out[None], latent_next)


def solution(mesh):
    halves, seq, columns = (mesh.shape[a] for a in ("cfg", "seq", "wt"))

    def run(*args):
        heads_here = args[6].shape[1] // columns // HD
        groups = math.gcd(heads_here, seq)
        fine = Mesh(
            mesh.devices.reshape(halves, groups, seq // groups, columns), ("cfg", "z", "t", "wt")
        )
        seq_axes = ("z", "t")
        weight = P(("cfg", "z", "t"), "wt")
        return jax.shard_map(
            on_device,
            mesh=fine,
            in_specs=(
                P("cfg", seq_axes, None),
                P(seq_axes, "cfg"),
                P(),
                P(seq_axes, None),
                P(None, "cfg", None, "wt"),
                P("cfg", None),
                weight,
                weight,
                weight,
                weight,
                weight,
                weight,
                P(),
                P(),
                P(),
            ),
            out_specs=(P("cfg", seq_axes, "wt"), P(seq_axes, "cfg")),
            check_vma=False,
        )(*args)

    return run
```

```python
import math

import jax
import jax.numpy as jnp
import numpy as np
from jax import lax
from jax.sharding import Mesh
from jax.sharding import PartitionSpec as P

HD = 128
TEXT = 512
TENANTS = 4
EPS = 1e-06
CHUNKS = 2
BF = jnp.bfloat16
F32 = jnp.float32


def flip(block, axis):
    return lax.ppermute(block, axis, [(0, 1), (1, 0)])


def rotary_tables():
    sixth = HD // 6
    table = np.zeros((3, HD), np.float32)
    lane = 0
    for column, span in enumerate((HD - 4 * sixth, 2 * sixth, 2 * sixth)):
        exponent = np.arange(0, span, 2).astype(np.float32) / np.float32(span)
        frequency = (1.0 / 10000.0**exponent).astype(np.float32)
        table[column, lane : lane + span] = np.repeat(frequency, 2)
        lane += span
    swap = np.zeros((HD, HD), np.float32)
    for pair in range(0, HD, 2):
        swap[pair + 1, pair] = -1.0
        swap[pair, pair + 1] = 1.0
    return table, swap


def head_scale(shaped):
    return lax.rsqrt(jnp.mean(shaped * shaped, axis=-1, keepdims=True) + EPS)


def attend(queries, keys, values, allowed):
    scores = jnp.einsum("qhd,khd->hqk", queries, keys, preferred_element_type=F32)
    scores = scores * (1.0 / math.sqrt(queries.shape[-1]))
    weights = jnp.where(allowed[None], jnp.exp(scores), 0.0).astype(BF)
    summed = jnp.einsum("hqk,khd->qhd", weights, values, preferred_element_type=F32)
    totals = jnp.sum(weights.astype(F32), axis=2).T
    return (summed / totals[..., None]).astype(BF).reshape(queries.shape[0], -1)


def on_device(
    hidden,
    latent,
    tenant_lengths,
    grid_positions,
    text_kv,
    text_lengths,
    w_query,
    w_key,
    w_value,
    w_out,
    w_cross_query,
    w_cross_out,
    w_head,
    guidance,
    step_size,
):
    halves, groups, parts, columns = (lax.axis_size(a) for a in ("cfg", "z", "t", "wt"))
    half_index, z_index, t_index, wt_index = (
        lax.axis_index(a) for a in ("cfg", "z", "t", "wt")
    )
    tok, width = hidden.shape[1:]
    rows = groups * tok
    local_cols = w_query.shape[1]
    my_cols = local_cols // groups
    heads = my_cols // HD
    paired = halves == 2 and parts == 2
    block = w_query.shape[0]
    ends = jnp.cumsum(tenant_lengths)

    def tenant_of(indices):
        return jnp.sum((indices[:, None] >= ends[None, :]).astype(jnp.int32), axis=1)

    def ordered(mine, other, index):
        return jnp.where(
            index == 0, jnp.concatenate([mine, other]), jnp.concatenate([other, mine])
        )

    def wide(w):
        if not paired:
            return lax.all_gather(w, ("cfg", "t"), axis=0, tiled=True)
        two = ordered(w, flip(w, "t"), t_index)
        return ordered(two, flip(two, "cfg"), half_index)

    def over_groups(x):
        return x if groups == 1 else lax.all_to_all(x, "z", 0, 0, tiled=True)

    def join_groups(x):
        if groups == 1:
            return x
        x = lax.all_gather(x, "z", axis=0)
        return jnp.swapaxes(x, 0, 1).reshape(x.shape[1], local_cols)

    def sum_at_owner(x):
        if groups == 1:
            return x[0].astype(F32)
        return jnp.sum(lax.all_to_all(x, "z", 0, 0).astype(F32), axis=0)

    def sum_groups(x):
        if groups == 1:
            return x
        return lax.psum_scatter(x, "z", scatter_dimension=0, tiled=True)

    def to_groups(x, n):
        return jnp.swapaxes(x.reshape(x.shape[0], groups, n), 0, 1)

    def both_columns(terms):
        terms = terms.astype(BF)
        if columns == 1:
            return terms.astype(F32)
        if columns == 2:
            return terms.astype(F32) + flip(terms, "wt").astype(F32)
        return lax.psum(terms, "wt").astype(F32)

    if paired:
        key_pair = ordered(w_key, flip(w_key, "t"), t_index)
        key_pair, w_query, w_value = lax.optimization_barrier((key_pair, w_query, w_value))
        wide_key = ordered(key_pair, flip(key_pair, "cfg"), half_index)
    else:
        wide_key = wide(w_key)
    wide_query, wide_value = wide(w_query), wide(w_value)
    wide_out, wide_cross, wide_cross_out = wide(w_out), wide(w_cross_query), wide(w_cross_out)

    chunks = CHUNKS if groups > 1 and tok % (CHUNKS * 16) == 0 else 1
    part = tok // chunks
    chunk_rows = rows // chunks

    def by_chunk(x):
        shape = (groups, chunks, part) + x.shape[2:]
        return jnp.swapaxes(x.reshape(shape), 0, 1).reshape((rows,) + x.shape[2:])

    def three_terms(x):
        high = lax.reduce_precision(x, 8, 7)
        middle = lax.reduce_precision(x - high, 8, 7)
        return [term.astype(BF) for term in (high, middle, x - high - middle)]

    own = hidden[0].astype(F32)
    mean = jnp.mean(own, axis=-1, keepdims=True)
    centred = own - mean
    scale = lax.rsqrt(jnp.mean(centred * centred, axis=-1, keepdims=True) + EPS)
    facts = jnp.concatenate([mean, scale, grid_positions.astype(F32)], axis=1)
    slice_width = width // groups
    if groups == 1:
        sliced = own
    else:
        extra = jnp.concatenate(three_terms(facts), axis=1)
        extra = jnp.pad(extra, ((0, 0), (0, 128 - extra.shape[1])))
        features = hidden[0].reshape(tok, halves, groups, slice_width // halves)
        features = jnp.concatenate(
            [features[:, half] for half in range(halves)]
            + [jnp.broadcast_to(extra[:, None], (tok, groups, 128))],
            axis=2,
        )
        arrived = lax.all_to_all(jnp.swapaxes(features, 0, 1), "z", 0, 0)
        arrived = by_chunk(arrived).astype(F32)
        sliced = arrived[:, :slice_width]
        extra = arrived[:, slice_width : slice_width + 15]
        facts = extra[:, 0:5] + extra[:, 5:10] + extra[:, 10:15]
    normed = ((sliced - facts[:, 0:1]) * facts[:, 1:2]).astype(BF)

    def project(w):
        return to_groups(jnp.dot(normed, w, preferred_element_type=F32).astype(BF), my_cols)

    projected_keys = sum_at_owner(project(wide_key)).astype(BF)
    projected = jnp.concatenate([project(wide_query), project(wide_value)], axis=2)
    projected = sum_groups(projected.reshape(groups * rows, 2 * my_cols))

    table, swap = rotary_tables()
    angles = (
        facts[:, 2:3] * table[0][None] + facts[:, 3:4] * table[1][None] + facts[:, 4:5] * table[2][None]
    )
    cosine, sinus = jnp.cos(angles)[:, None, :], jnp.sin(angles)[:, None, :]

    def rotated(x):
        shaped = x.reshape(rows, heads, HD)
        swapped = jnp.einsum("thd,de->the", shaped, jnp.asarray(swap, BF), preferred_element_type=F32)
        shaped = shaped.astype(F32)
        return ((shaped * cosine + swapped * sinus) * head_scale(shaped)).astype(BF)

    keys = rotated(projected_keys).reshape(rows, my_cols)
    queries = rotated(projected[:, :my_cols])
    values = projected[:, my_cols:]

    base = jnp.arange(groups, dtype=jnp.int32)[:, None] * (parts * tok)
    base = by_chunk(base + jnp.arange(tok, dtype=jnp.int32)[None])
    my_tenant = tenant_of(base + t_index * tok)
    if parts == 2:
        keys = jnp.concatenate([keys, flip(keys, "t")], axis=0)
        values = jnp.concatenate([values, flip(values, "t")], axis=0)
        key_tenant = jnp.concatenate([my_tenant, tenant_of(base + (1 - t_index) * tok)])
    else:
        keys = lax.all_gather(keys, "t", axis=0, tiled=True)
        values = lax.all_gather(values, "t", axis=0, tiled=True)
        key_tenant = tenant_of(
            (jnp.arange(parts, dtype=jnp.int32)[:, None] * tok + base[None]).reshape(-1)
        )
    keys = keys.reshape(-1, heads, HD)
    values = values.reshape(-1, heads, HD)

    spans = [slice(i * chunk_rows, (i + 1) * chunk_rows) for i in range(chunks)]
    mixed = [
        attend(queries[i], keys, values, my_tenant[i][:, None] == key_tenant[None, :])
        for i in spans
    ]

    def project_out(mixed, weight):
        return lax.dot_general(
            join_groups(mixed), weight, (((1,), (1,)), ((), ())), preferred_element_type=F32
        )

    column_sums = jnp.dot(jnp.ones((8, slice_width), BF), wide_cross, preferred_element_type=F32)
    column_sums = column_sums[0].reshape(groups, 1, my_cols)
    riding = groups > 1 and chunk_rows <= my_cols

    text = lax.dynamic_slice_in_dim(text_kv[:, 0], z_index * my_cols, my_cols, 2)
    text_keys = text[0].reshape(-1, heads, HD).astype(F32)
    text_keys = (text_keys * head_scale(text_keys)).astype(BF)
    text_values = text[1].reshape(-1, heads, HD)
    text_index = jnp.arange(text_kv.shape[2], dtype=jnp.int32)
    text_tenant = text_index // TEXT
    slots = text_tenant[:, None] == jnp.arange(TENANTS, dtype=jnp.int32)[None, :]
    live_length = jnp.sum(jnp.where(slots, text_lengths[0][None, :], 0), axis=1)
    live = text_index % TEXT < live_length

    states, cross_mixed = [], []
    for i, block_mixed in zip(spans, mixed):
        shifted = (sliced[i] - facts[i, 0:1]) + both_columns(project_out(block_mixed, wide_out))
        states.append(shifted)
        sums = jnp.stack([jnp.sum(shifted, axis=1), jnp.sum(shifted * shifted, axis=1)])
        crossed = jnp.dot(shifted.astype(BF), wide_cross, preferred_element_type=F32).astype(BF)
        crossed = to_groups(crossed, my_cols)
        if riding:
            sums = jnp.concatenate(three_terms(sums))
            sums = jnp.pad(sums, ((0, 0), (0, my_cols - chunk_rows)))
            sums = jnp.broadcast_to(sums[None], (groups,) + sums.shape)
            below = jnp.concatenate([sums] + three_terms(column_sums), axis=1)
            below = jnp.pad(below, ((0, 0), (0, 16 - below.shape[1]), (0, 0)))
            arrived = sum_at_owner(jnp.concatenate([crossed, below], axis=1))
            crossed, below = arrived[:chunk_rows], arrived[chunk_rows:]
            sums = (below[0:2] + below[2:4] + below[4:6])[:, :chunk_rows]
            all_columns = below[6:7] + below[7:8] + below[8:9]
        else:
            sums = sum_at_owner(jnp.broadcast_to(sums[None], (groups,) + sums.shape))
            all_columns = sum_at_owner(column_sums)
            crossed = sum_at_owner(crossed)
        sums = sums / width
        variance = jnp.maximum(sums[1] - sums[0] * sums[0], 0.0)[:, None, None]
        shaped = (crossed - sums[0][:, None] * all_columns).reshape(chunk_rows, heads, HD)
        square = jnp.mean(shaped * shaped, axis=-1, keepdims=True)
        cross_queries = (shaped * lax.rsqrt(square + EPS * (variance + EPS))).astype(BF)
        allowed = (my_tenant[i][:, None] == text_tenant[None, :]) & live[None]
        cross_mixed.append(attend(cross_queries, text_keys, text_values, allowed))

    channels = w_head.shape[1]
    head_rows = lax.dynamic_index_in_dim(
        w_head.reshape(halves, groups, parts * block, channels), z_index, 1, keepdims=False
    ).reshape(-1, channels)
    totals = jnp.sum(w_head.astype(F32), axis=0)[None]
    out_width = width // columns

    leaving, sums = [], []
    for i, shifted, block_mixed in zip(spans, states, cross_mixed):
        shifted = shifted + both_columns(project_out(block_mixed, wide_cross_out))
        final = (shifted + facts[i, 0:1]).astype(BF)
        if groups > 1 and columns == halves:
            span = slice_width // halves
            final = lax.dynamic_slice_in_dim(final, wt_index * span, span, 1)
        leaving.append(final.reshape(groups, part, -1))
        some = jnp.concatenate(
            [
                jnp.dot(shifted.astype(BF), head_rows, preferred_element_type=F32),
                jnp.sum(shifted, axis=1, keepdims=True),
                jnp.sum(shifted * shifted, axis=1, keepdims=True),
            ],
            axis=1,
        )
        sums.append(some.reshape(groups, part, channels + 2))
    sums = sum_at_owner(jnp.concatenate(sums, axis=1))
    mean = sums[:, channels : channels + 1] / width
    variance = jnp.maximum(sums[:, channels + 1 :] / width - mean * mean, 0.0)
    velocity = (sums[:, :channels] - mean * totals) * lax.rsqrt(variance + EPS)

    leaving = jnp.concatenate(leaving, axis=1)
    if groups == 1:
        hidden_out = lax.dynamic_slice_in_dim(leaving[0], wt_index * out_width, out_width, 1)
    else:
        leaving = jnp.swapaxes(lax.all_to_all(leaving, "z", 0, 0), 0, 1)
        if columns == halves:
            hidden_out = leaving.reshape(tok, out_width)
        else:
            leaving = jnp.swapaxes(leaving.reshape(tok, groups, halves, -1), 1, 2)
            hidden_out = lax.dynamic_slice_in_dim(
                leaving.reshape(tok, width), wt_index * out_width, out_width, 1
            )

    channel_half = latent.shape[1]
    outgoing = lax.dynamic_slice_in_dim(velocity, (1 - half_index) * channel_half, channel_half, 1)
    partner = flip(outgoing, "cfg")
    own_part = lax.dynamic_slice_in_dim(velocity, half_index * channel_half, channel_half, 1)
    conditional = jnp.where(half_index == 0, own_part, partner)
    null_text = jnp.where(half_index == 0, partner, own_part)
    latent_next = latent + step_size[0] * (null_text + guidance[0] * (conditional - null_text))
    return (hidden_out[None], latent_next)


def solution(mesh):
    halves, seq, columns = (mesh.shape[a] for a in ("cfg", "seq", "wt"))

    def run(*args):
        heads_here = args[6].shape[1] // columns // HD
        groups = math.gcd(heads_here, seq)
        fine = Mesh(
            mesh.devices.reshape(halves, groups, seq // groups, columns), ("cfg", "z", "t", "wt")
        )
        seq_axes = ("z", "t")
        weight = P(("cfg", "z", "t"), "wt")
        return jax.shard_map(
            on_device,
            mesh=fine,
            in_specs=(
                P("cfg", seq_axes, None),
                P(seq_axes, "cfg"),
                P(),
                P(seq_axes, None),
                P(None, "cfg", None, "wt"),
                P("cfg", None),
                weight,
                weight,
                weight,
                weight,
                weight,
                weight,
                P(),
                P(),
                P(),
            ),
            out_specs=(P("cfg", seq_axes, "wt"), P(seq_axes, "cfg")),
            check_vma=False,
        )(*args)

    return run
```

```python
import math

import jax
import jax.numpy as jnp
import numpy as np
from jax import lax
from jax.sharding import Mesh
from jax.sharding import PartitionSpec as P

HD = 128
TEXT = 512
TENANTS = 4
EPS = 1e-06
CHUNKS = 2
BF = jnp.bfloat16
F32 = jnp.float32


def flip(block, axis):
    return lax.ppermute(block, axis, [(0, 1), (1, 0)])


def rotary_tables():
    sixth = HD // 6
    table = np.zeros((3, HD), np.float32)
    lane = 0
    for column, span in enumerate((HD - 4 * sixth, 2 * sixth, 2 * sixth)):
        exponent = np.arange(0, span, 2).astype(np.float32) / np.float32(span)
        frequency = (1.0 / 10000.0**exponent).astype(np.float32)
        table[column, lane : lane + span] = np.repeat(frequency, 2)
        lane += span
    swap = np.zeros((HD, HD), np.float32)
    for pair in range(0, HD, 2):
        swap[pair + 1, pair] = -1.0
        swap[pair, pair + 1] = 1.0
    return table, swap


def head_scale(shaped):
    return lax.rsqrt(jnp.mean(shaped * shaped, axis=-1, keepdims=True) + EPS)


def attend(queries, keys, values, allowed):
    scores = jnp.einsum("qhd,khd->hqk", queries, keys, preferred_element_type=F32)
    scores = scores * (1.0 / math.sqrt(queries.shape[-1]))
    weights = jnp.where(allowed[None], jnp.exp(scores), 0.0).astype(BF)
    summed = jnp.einsum("hqk,khd->qhd", weights, values, preferred_element_type=F32)
    totals = jnp.sum(weights.astype(F32), axis=2).T
    return (summed / totals[..., None]).astype(BF).reshape(queries.shape[0], -1)


def on_device(
    hidden,
    latent,
    tenant_lengths,
    grid_positions,
    text_kv,
    text_lengths,
    w_query,
    w_key,
    w_value,
    w_out,
    w_cross_query,
    w_cross_out,
    w_head,
    guidance,
    step_size,
):
    halves, groups, parts, columns = (lax.axis_size(a) for a in ("cfg", "z", "t", "wt"))
    half_index, z_index, t_index, wt_index = (
        lax.axis_index(a) for a in ("cfg", "z", "t", "wt")
    )
    tok, width = hidden.shape[1:]
    rows = groups * tok
    local_cols = w_query.shape[1]
    my_cols = local_cols // groups
    heads = my_cols // HD
    paired = halves == 2 and parts == 2
    block = w_query.shape[0]
    ends = jnp.cumsum(tenant_lengths)

    def tenant_of(indices):
        return jnp.sum((indices[:, None] >= ends[None, :]).astype(jnp.int32), axis=1)

    def ordered(mine, other, index):
        return jnp.where(
            index == 0, jnp.concatenate([mine, other]), jnp.concatenate([other, mine])
        )

    def wide(w):
        if not paired:
            return lax.all_gather(w, ("cfg", "t"), axis=0, tiled=True)
        two = ordered(w, flip(w, "t"), t_index)
        return ordered(two, flip(two, "cfg"), half_index)

    def over_groups(x):
        return x if groups == 1 else lax.all_to_all(x, "z", 0, 0, tiled=True)

    def join_groups(x):
        if groups == 1:
            return x
        x = lax.all_gather(x, "z", axis=0)
        return jnp.swapaxes(x, 0, 1).reshape(x.shape[1], local_cols)

    def sum_at_owner(x):
        if groups == 1:
            return x[0].astype(F32)
        return jnp.sum(lax.all_to_all(x, "z", 0, 0).astype(F32), axis=0)

    def sum_groups(x):
        if groups == 1:
            return x
        return lax.psum_scatter(x, "z", scatter_dimension=0, tiled=True)

    def to_groups(x, n):
        return jnp.swapaxes(x.reshape(x.shape[0], groups, n), 0, 1)

    def both_columns(terms):
        terms = terms.astype(BF)
        if columns == 1:
            return terms.astype(F32)
        if columns == 2:
            return terms.astype(F32) + flip(terms, "wt").astype(F32)
        return lax.psum(terms, "wt").astype(F32)

    if paired:
        key_pair = ordered(w_key, flip(w_key, "t"), t_index)
        key_pair, w_query, w_value = lax.optimization_barrier((key_pair, w_query, w_value))
        wide_key = ordered(key_pair, flip(key_pair, "cfg"), half_index)
    else:
        wide_key = wide(w_key)
    wide_query, wide_value = wide(w_query), wide(w_value)
    wide_out, wide_cross, wide_cross_out = wide(w_out), wide(w_cross_query), wide(w_cross_out)

    chunks = CHUNKS if groups > 1 and tok % (CHUNKS * 16) == 0 else 1
    part = tok // chunks
    chunk_rows = rows // chunks

    def by_chunk(x):
        shape = (groups, chunks, part) + x.shape[2:]
        return jnp.swapaxes(x.reshape(shape), 0, 1).reshape((rows,) + x.shape[2:])

    def three_terms(x):
        high = lax.reduce_precision(x, 8, 7)
        middle = lax.reduce_precision(x - high, 8, 7)
        return [term.astype(BF) for term in (high, middle, x - high - middle)]

    own = hidden[0].astype(F32)
    mean = jnp.mean(own, axis=-1, keepdims=True)
    centred = own - mean
    scale = lax.rsqrt(jnp.mean(centred * centred, axis=-1, keepdims=True) + EPS)
    facts = jnp.concatenate([mean, scale, grid_positions.astype(F32)], axis=1)
    slice_width = width // groups
    if groups == 1:
        sliced = own
    else:
        extra = jnp.concatenate(three_terms(facts), axis=1)
        extra = jnp.pad(extra, ((0, 0), (0, 128 - extra.shape[1])))
        features = hidden[0].reshape(tok, halves, groups, slice_width // halves)
        features = jnp.concatenate(
            [features[:, half] for half in range(halves)]
            + [jnp.broadcast_to(extra[:, None], (tok, groups, 128))],
            axis=2,
        )
        arrived = lax.all_to_all(jnp.swapaxes(features, 0, 1), "z", 0, 0)
        arrived = by_chunk(arrived).astype(F32)
        sliced = arrived[:, :slice_width]
        extra = arrived[:, slice_width : slice_width + 15]
        facts = extra[:, 0:5] + extra[:, 5:10] + extra[:, 10:15]
    normed = ((sliced - facts[:, 0:1]) * facts[:, 1:2]).astype(BF)

    def project(normed, w):
        return to_groups(jnp.dot(normed, w, preferred_element_type=F32).astype(BF), my_cols)

    projected_keys, normed = lax.optimization_barrier((project(normed, wide_key), normed))
    projected_keys = sum_at_owner(projected_keys).astype(BF)
    projected = jnp.concatenate([project(normed, wide_query), project(normed, wide_value)], axis=2)
    projected = sum_groups(projected.reshape(groups * rows, 2 * my_cols))

    table, swap = rotary_tables()
    angles = (
        facts[:, 2:3] * table[0][None] + facts[:, 3:4] * table[1][None] + facts[:, 4:5] * table[2][None]
    )
    cosine, sinus = jnp.cos(angles)[:, None, :], jnp.sin(angles)[:, None, :]

    def rotated(x):
        shaped = x.reshape(rows, heads, HD)
        swapped = jnp.einsum("thd,de->the", shaped, jnp.asarray(swap, BF), preferred_element_type=F32)
        shaped = shaped.astype(F32)
        return ((shaped * cosine + swapped * sinus) * head_scale(shaped)).astype(BF)

    keys = rotated(projected_keys).reshape(rows, my_cols)
    queries = rotated(projected[:, :my_cols])
    values = projected[:, my_cols:]

    base = jnp.arange(groups, dtype=jnp.int32)[:, None] * (parts * tok)
    base = by_chunk(base + jnp.arange(tok, dtype=jnp.int32)[None])
    my_tenant = tenant_of(base + t_index * tok)
    if parts == 2:
        keys = jnp.concatenate([keys, flip(keys, "t")], axis=0)
        values = jnp.concatenate([values, flip(values, "t")], axis=0)
        key_tenant = jnp.concatenate([my_tenant, tenant_of(base + (1 - t_index) * tok)])
    else:
        keys = lax.all_gather(keys, "t", axis=0, tiled=True)
        values = lax.all_gather(values, "t", axis=0, tiled=True)
        key_tenant = tenant_of(
            (jnp.arange(parts, dtype=jnp.int32)[:, None] * tok + base[None]).reshape(-1)
        )
    keys = keys.reshape(-1, heads, HD)
    values = values.reshape(-1, heads, HD)

    spans = [slice(i * chunk_rows, (i + 1) * chunk_rows) for i in range(chunks)]
    mixed = [
        attend(queries[i], keys, values, my_tenant[i][:, None] == key_tenant[None, :])
        for i in spans
    ]

    def project_out(mixed, weight):
        return lax.dot_general(
            join_groups(mixed), weight, (((1,), (1,)), ((), ())), preferred_element_type=F32
        )

    column_sums = jnp.dot(jnp.ones((8, slice_width), BF), wide_cross, preferred_element_type=F32)
    column_sums = column_sums[0].reshape(groups, 1, my_cols)
    riding = groups > 1 and chunk_rows <= my_cols

    text = lax.dynamic_slice_in_dim(text_kv[:, 0], z_index * my_cols, my_cols, 2)
    text_keys = text[0].reshape(-1, heads, HD).astype(F32)
    text_keys = (text_keys * head_scale(text_keys)).astype(BF)
    text_values = text[1].reshape(-1, heads, HD)
    text_index = jnp.arange(text_kv.shape[2], dtype=jnp.int32)
    text_tenant = text_index // TEXT
    slots = text_tenant[:, None] == jnp.arange(TENANTS, dtype=jnp.int32)[None, :]
    live_length = jnp.sum(jnp.where(slots, text_lengths[0][None, :], 0), axis=1)
    live = text_index % TEXT < live_length

    states, cross_mixed = [], []
    for i, block_mixed in zip(spans, mixed):
        shifted = (sliced[i] - facts[i, 0:1]) + both_columns(project_out(block_mixed, wide_out))
        states.append(shifted)
        sums = jnp.stack([jnp.sum(shifted, axis=1), jnp.sum(shifted * shifted, axis=1)])
        crossed = jnp.dot(shifted.astype(BF), wide_cross, preferred_element_type=F32).astype(BF)
        crossed = to_groups(crossed, my_cols)
        if riding:
            sums = jnp.concatenate(three_terms(sums))
            sums = jnp.pad(sums, ((0, 0), (0, my_cols - chunk_rows)))
            sums = jnp.broadcast_to(sums[None], (groups,) + sums.shape)
            below = jnp.concatenate([sums] + three_terms(column_sums), axis=1)
            below = jnp.pad(below, ((0, 0), (0, 16 - below.shape[1]), (0, 0)))
            arrived = sum_at_owner(jnp.concatenate([crossed, below], axis=1))
            crossed, below = arrived[:chunk_rows], arrived[chunk_rows:]
            sums = (below[0:2] + below[2:4] + below[4:6])[:, :chunk_rows]
            all_columns = below[6:7] + below[7:8] + below[8:9]
        else:
            sums = sum_at_owner(jnp.broadcast_to(sums[None], (groups,) + sums.shape))
            all_columns = sum_at_owner(column_sums)
            crossed = sum_at_owner(crossed)
        sums = sums / width
        variance = jnp.maximum(sums[1] - sums[0] * sums[0], 0.0)[:, None, None]
        shaped = (crossed - sums[0][:, None] * all_columns).reshape(chunk_rows, heads, HD)
        square = jnp.mean(shaped * shaped, axis=-1, keepdims=True)
        cross_queries = (shaped * lax.rsqrt(square + EPS * (variance + EPS))).astype(BF)
        allowed = (my_tenant[i][:, None] == text_tenant[None, :]) & live[None]
        cross_mixed.append(attend(cross_queries, text_keys, text_values, allowed))

    channels = w_head.shape[1]
    head_rows = lax.dynamic_index_in_dim(
        w_head.reshape(halves, groups, parts * block, channels), z_index, 1, keepdims=False
    ).reshape(-1, channels)
    totals = jnp.sum(w_head.astype(F32), axis=0)[None]
    out_width = width // columns

    leaving, sums = [], []
    for i, shifted, block_mixed in zip(spans, states, cross_mixed):
        shifted = shifted + both_columns(project_out(block_mixed, wide_cross_out))
        final = (shifted + facts[i, 0:1]).astype(BF)
        if groups > 1 and columns == halves:
            span = slice_width // halves
            final = lax.dynamic_slice_in_dim(final, wt_index * span, span, 1)
        leaving.append(final.reshape(groups, part, -1))
        some = jnp.concatenate(
            [
                jnp.dot(shifted.astype(BF), head_rows, preferred_element_type=F32),
                jnp.sum(shifted, axis=1, keepdims=True),
                jnp.sum(shifted * shifted, axis=1, keepdims=True),
            ],
            axis=1,
        )
        sums.append(some.reshape(groups, part, channels + 2))
    sums = jnp.concatenate(sums, axis=1)
    leaving = jnp.concatenate(leaving, axis=1)
    if groups == 1:
        sums = sums[0]
    else:
        facts_width = 3 * (channels + 2)
        pad = -facts_width % 128
        wide_row = leaving.shape[2]
        leaving = jnp.concatenate([leaving] + three_terms(sums), axis=2)
        leaving = lax.all_to_all(jnp.pad(leaving, ((0, 0), (0, 0), (0, pad))), "z", 0, 0)
        sums = jnp.sum(leaving[:, :, wide_row:].astype(F32), axis=0)
        sums = sum(sums[:, i * (channels + 2) : (i + 1) * (channels + 2)] for i in range(3))
        leaving = jnp.swapaxes(leaving[:, :, :wide_row], 0, 1)
    mean = sums[:, channels : channels + 1] / width
    variance = jnp.maximum(sums[:, channels + 1 :] / width - mean * mean, 0.0)
    velocity = (sums[:, :channels] - mean * totals) * lax.rsqrt(variance + EPS)

    if groups == 1:
        hidden_out = lax.dynamic_slice_in_dim(leaving[0], wt_index * out_width, out_width, 1)
    else:
        if columns == halves:
            hidden_out = leaving.reshape(tok, out_width)
        else:
            leaving = jnp.swapaxes(leaving.reshape(tok, groups, halves, -1), 1, 2)
            hidden_out = lax.dynamic_slice_in_dim(
                leaving.reshape(tok, width), wt_index * out_width, out_width, 1
            )

    channel_half = latent.shape[1]
    outgoing = lax.dynamic_slice_in_dim(velocity, (1 - half_index) * channel_half, channel_half, 1)
    partner = flip(outgoing, "cfg")
    own_part = lax.dynamic_slice_in_dim(velocity, half_index * channel_half, channel_half, 1)
    conditional = jnp.where(half_index == 0, own_part, partner)
    null_text = jnp.where(half_index == 0, partner, own_part)
    latent_next = latent + step_size[0] * (null_text + guidance[0] * (conditional - null_text))
    return (hidden_out[None], latent_next)


def solution(mesh):
    halves, seq, columns = (mesh.shape[a] for a in ("cfg", "seq", "wt"))

    def run(*args):
        heads_here = args[6].shape[1] // columns // HD
        groups = math.gcd(heads_here, seq)
        fine = Mesh(
            mesh.devices.reshape(halves, groups, seq // groups, columns), ("cfg", "z", "t", "wt")
        )
        seq_axes = ("z", "t")
        weight = P(("cfg", "z", "t"), "wt")
        return jax.shard_map(
            on_device,
            mesh=fine,
            in_specs=(
                P("cfg", seq_axes, None),
                P(seq_axes, "cfg"),
                P(),
                P(seq_axes, None),
                P(None, "cfg", None, "wt"),
                P("cfg", None),
                weight,
                weight,
                weight,
                weight,
                weight,
                weight,
                P(),
                P(),
                P(),
            ),
            out_specs=(P("cfg", seq_axes, "wt"), P(seq_axes, "cfg")),
            check_vma=False,
        )(*args)

    return run
```
